512 devices in a mesh: ep: 128 (over z, x, core), dp: 4 (over y).
Axes of the slice: x: 4, y: 4, z: 16, core: 2. Of those that a mesh axis runs over, the one named last changes fastest.
Arguments:
- tokens: bfloat16 [512, 4096], P(('dp', 'ep')), parts along dimension 0, may hold values from -6 to 6
- expert_ids: int32 [512, 8], P(('dp', 'ep')), parts along dimension 0, may hold values from 0 to 15, as said below
- gates: float32 [512, 8], P(('dp', 'ep')), parts along dimension 0, may hold values from 0.1 to 1
- gate_weight: bfloat16 [128, 192, 4096], P('ep'), may hold values from -0.09375 to 0.09375
- up_weight: bfloat16 [128, 192, 4096], P('ep'), may hold values from -0.09375 to 0.09375
- down_weight: bfloat16 [128, 192, 4096], P('ep'), may hold values from -0.15625 to 0.15625
Outputs:
- combined: bfloat16 [512, 4096], P(('dp', 'ep')), parts along dimension 0
The draws below stay inside these ranges and needn't reach their ends.
There are 4 independent parts, one for each index of `dp`. The reference program is written for one: setup_inputs(seed, part) draws one part's arguments, and reference() takes and returns one part's arrays. A program takes and returns all parts, laid end to end along the dimension named above; an argument that names none is the same for every part. Nothing has to cross between parts.
Inputs may be any that keep to these rules, and one draw needn't show every extreme that they name: `expert_ids`: each row names 8 different experts.
All inputs are finite; a program needn't handle non-finite values.
Results may differ from the reference program's by a relative error of at most 0.012.
Values may be sent and summed in bfloat16 or wider, within the bound.
A program may use at most 64 MiB of HBM per device.

```python
import math
import jax
import jax.numpy as jnp
from jax import lax

D = 4096
HIDDEN_SIZE = 1536
HID_DEV = 192
EXPERTS = 16
TOP = 8
TOK_DEV = 1
TOKENS = 128
N_EP = 128


def draw_expert_ids(key, part):
    key_offset = jax.random.fold_in(key, 101)
    key_hot = jax.random.fold_in(key, 102)
    key_perm = jax.random.fold_in(key, 103)
    key_rotation = jax.random.fold_in(key, 104)
    owners = TOKENS // TOK_DEV
    offset = jax.random.randint(key_offset, (), 0, EXPERTS)
    hot_expert = (offset + jax.random.randint(key_hot, (owners,), 0, 4)) % EXPERTS
    hot_rows = jnp.repeat(hot_expert, TOK_DEV)
    row_keys = jax.random.split(key_perm, TOKENS)
    shuffled = jax.vmap(lambda row_key: jax.random.permutation(row_key, max(EXPERTS - 1, 1)))(row_keys)
    rest_ids = (hot_rows[:, None] + 1 + shuffled[:, :TOP - 1]) % EXPERTS
    route_ids = jnp.concatenate([hot_rows[:, None], rest_ids], axis=1)
    rotation = jax.random.randint(key_rotation, (TOKENS, 1), 0, TOP)
    col_order = (jnp.arange(TOP)[None, :] + rotation) % TOP
    route_ids = jnp.take_along_axis(route_ids, col_order, axis=1)
    return route_ids.astype(jnp.int32)


def block_levels(rng, extent, shards, least, largest):
    def one(dim, blocks):
        steps = jax.random.uniform(jax.random.fold_in(jax.random.fold_in(rng, 6), dim), (blocks,), jnp.float32, least / len(shards), largest / len(shards))
        return jnp.repeat(jnp.exp(steps), extent[dim] // blocks).reshape((-1,) + (1,) * (len(extent) - dim - 1))

    level = one(*shards[0])
    for cut in shards[1:]:
        level = level * one(*cut)
    return level


def gaussian(key, shape, width, limit, pieces=(), held_as=jnp.bfloat16):
    result = jax.random.normal(key, shape, jnp.float32) * width
    if len(pieces) > 0:
        result = block_levels(key, shape, pieces, -0.22, 0.18) * result
    return jnp.clip(result, min=-limit, max=limit).astype(held_as)


def setup_inputs(seed: int = 0, part: int = 0) -> dict:
    key_list = jax.random.split(jax.random.key(seed), 7)
    part_keys = jax.random.split(jax.random.fold_in(key_list[6], part), 7)
    tokens = gaussian(part_keys[0], (TOKENS, D), 1.0, 6.0, ((0, 128),))
    expert_ids = draw_expert_ids(jax.random.fold_in(jax.random.fold_in(key_list[6], part), 71), part)
    gates = jnp.clip(jnp.exp(math.log(1.0) - 2.3025851 * jax.random.uniform(part_keys[2], (TOKENS, TOP), jnp.float32) ** block_levels(part_keys[2], (TOKENS, TOP), ((0, 128),), -0.2, 0.2)), 0.1, 1.0)
    gate_weight = gaussian(key_list[3], (N_EP, HID_DEV, D), D ** -0.5, 0.09375, ((0, 128),))
    up_weight = gaussian(key_list[4], (N_EP, HID_DEV, D), D ** -0.5, 0.09375, ((0, 128),))
    down_weight = gaussian(key_list[5], (N_EP, HID_DEV, D), HIDDEN_SIZE ** -0.5, 0.15625, ((0, 128),))
    return {"tokens": tokens, "expert_ids": expert_ids, "gates": gates, "gate_weight": gate_weight, "up_weight": up_weight, "down_weight": down_weight}


def expert(operands):
    rows_in, w_gate, w_up, w_down = operands
    dims = (((1,), (1,)), ((), ()))
    gate_act = lax.dot_general(rows_in, w_gate, dims, preferred_element_type=jnp.float32)
    up_act = lax.dot_general(rows_in, w_up, dims, preferred_element_type=jnp.float32)
    hidden = (jax.nn.silu(gate_act) * up_act).astype(jnp.bfloat16)
    return jnp.dot(hidden, w_down, preferred_element_type=jnp.float32).astype(jnp.bfloat16)


def reference(tokens, expert_ids, gates, gate_weight, up_weight, down_weight):
    all_rows = tokens.shape[0]
    cap_place = jnp.arange(all_rows, dtype=jnp.int32)
    spread = jnp.broadcast_to(tokens[:, None, :], (all_rows, TOP, D))
    buffer = jnp.zeros((EXPERTS, all_rows, D), tokens.dtype).at[expert_ids, cap_place[:, None]].set(spread)
    gate_full = gate_weight.reshape(EXPERTS, HIDDEN_SIZE, D)
    up_full = up_weight.reshape(EXPERTS, HIDDEN_SIZE, D)
    down_full = down_weight.reshape(EXPERTS, HIDDEN_SIZE, D)
    outputs = lax.map(expert, (buffer, gate_full, up_full, down_full))
    picked = outputs[expert_ids, cap_place[:, None]].astype(jnp.float32)
    combined = jnp.einsum('rk,rkd->rd', gates.astype(jnp.float32), picked)
    return combined.astype(jnp.bfloat16)
```

```python
import functools

import jax
import jax.numpy as jnp
from jax import lax
from jax.experimental import pallas as pl
from jax.experimental.pallas import tpu as pltpu
from jax.sharding import PartitionSpec as P

MESH = pl.DeviceIdType.MESH
F32 = jnp.float32
BF16 = jnp.bfloat16
NZ, NX, NC = 16, 4, 2
SUB, LANE = 32, 128

K_OF = [k for j in range(1, 8) for k in (j, NZ - j)] + [8, 0]
P_OF = {k: p for p, k in enumerate(K_OF)}
NEAR = [(15, 1)] + [(2 * j, 2) for j in range(7)] + [(14, 1)]
FAR = NEAR[::-1]


def kernel(
    tok_ref, ids_ref, gate_ref, wg_hbm, wu_hbm, wd_hbm, out_ref,
    wg, wu, wd, own, got, meta, stage, rows, core_out, core_in, x_out, x_in, x_own, z_out, z_in,
    w_sem, az_s, az_r, am_s, am_r, ax_s, ax_r, ac_s, ac_r, rc_s, rc_r, rx_s, rx_r, rz_s, rz_r,
):
    me = lax.axis_index("ep")
    core = lax.rem(me, NC)
    x = lax.rem(me // NC, NX)
    z = me // (NC * NX)

    def device(dz, dx, dc):
        pz = lax.rem(z + dz, NZ)
        px = lax.rem(x + dx, NX)
        pc = lax.rem(core + dc, NC)
        return {"ep": (pz * NX + px) * NC + pc}

    def send(src, dst, s_sem, r_sem, to):
        copy = pltpu.make_async_remote_copy(
            src_ref=src, dst_ref=dst, send_sem=s_sem, recv_sem=r_sem, device_id=to, device_id_type=MESH
        )
        copy.start()
        return copy

    loads = []
    for n, (src, dst) in enumerate(((wg_hbm, wg), (wu_hbm, wu), (wd_hbm, wd))):
        copy = pltpu.make_async_copy(src.at[0], dst, w_sem.at[n])
        copy.start()
        loads.append(copy)

    peers = [device(k, 0, 0) for k in range(1, NZ)] + [device(0, k, 0) for k in range(1, NX)] + [device(0, 0, 1)]
    barrier = pltpu.get_barrier_semaphore()
    for peer in peers:
        pl.semaphore_signal(barrier, inc=1, device_id=peer, device_id_type=MESH)

    lane = lax.broadcasted_iota(jnp.int32, (1, LANE), 1)
    row = tok_ref[...].astype(F32)
    for j in range(SUB):
        stage[j : j + 1, :] = row[:, j * LANE : (j + 1) * LANE]
    own_row = stage[0:SUB, :].astype(BF16)
    own[...] = own_row
    got[0, 15, 0] = own_row
    weight = jnp.zeros((1, LANE), F32)
    for k in range(ids_ref.shape[1]):
        weight += jnp.where(lane == ids_ref[:, k : k + 1], gate_ref[:, k : k + 1], 0.0)
    meta[15] = weight

    pl.semaphore_wait(barrier, len(peers))

    sends = []
    for d in sorted(range(1, NZ), key=lambda d: -min(d, NZ - d)):
        p = P_OF[NZ - d]
        sends.append(send(own, got.at[0, p, 0], az_s.at[p], az_r.at[p], device(d, 0, 0)))
    for d in sorted(range(1, NZ), key=lambda d: -min(d, NZ - d)):
        p = P_OF[NZ - d]
        sends.append(send(meta.at[15], meta.at[p], am_s.at[p], am_r.at[p], device(d, 0, 0)))

    def take(dst, r_sem):
        pltpu.make_async_copy(dst, dst, r_sem).wait()

    def rows_along_x(g):
        p, n = NEAR[g]
        if g > 0:
            for q in range(p, p + n):
                take(got.at[0, q, 0], az_r.at[q])
        for d in range(1, NX):
            sends.append(
                send(
                    got.at[0, pl.ds(p, n), 0], got.at[0, pl.ds(p, n), NX - d],
                    ax_s.at[g, d - 1], ax_r.at[g, NX - d - 1], device(0, d, 0),
                )
            )

    def rows_to_partner(g):
        p, n = NEAR[g]
        for d in range(1, NX):
            take(got.at[0, pl.ds(p, n), d], ax_r.at[g, d - 1])
        sends.append(send(got.at[0, pl.ds(p, n)], got.at[1, pl.ds(p, n)], ac_s.at[g], ac_r.at[g], device(0, 0, 1)))

    def unpack(side, unit):
        base = side * 64 + unit * 16
        stage[pl.ds(base * SUB, 16 * SUB), :] = (
            got[side, 4 * unit : 4 * unit + 4].astype(F32).reshape(16 * SUB, LANE)
        )
        for j in range(SUB):
            rows[pl.ds(base, 16), j * LANE : (j + 1) * LANE] = stage[
                pl.ds(base * SUB + j, 16, stride=SUB), :
            ].astype(BF16)

    lag = 4
    for g in range(9 + lag):
        if g < 9:
            rows_along_x(g)
        if g >= lag:
            rows_to_partner(g - lag)
    for unit in range(4):
        unpack(0, unit)
    for unit in range(4):
        for g, (p, n) in enumerate(NEAR):
            if p // 4 == unit:
                take(got.at[1, pl.ds(p, n)], ac_r.at[g])
        unpack(1, unit)

    for copy in loads:
        copy.wait()
    contract = (((1,), (1,)), ((), ()))
    gate_act = lax.dot_general(rows[...], wg[...], contract, preferred_element_type=F32)
    up_act = lax.dot_general(rows[...], wu[...], contract, preferred_element_type=F32)
    hidden = (jax.nn.silu(gate_act) * up_act).astype(BF16)
    for n in range(16):
        value = jnp.dot(hidden, wd[:, n * 256 : (n + 1) * 256], preferred_element_type=F32)
        stage[pl.ds(2 * n, 128, stride=SUB), :] = value[:, :LANE]
        stage[pl.ds(2 * n + 1, 128, stride=SUB), :] = value[:, LANE:]

    for g, (p, n) in enumerate(FAR):
        core_out[pl.ds(p, n)] = (
            stage[pl.ds((64 + p * 4) * SUB, n * 4 * SUB), :].astype(BF16).reshape(n, NX, SUB, LANE)
        )
        sends.append(send(core_out.at[pl.ds(p, n)], core_in.at[pl.ds(p, n)], rc_s.at[g], rc_r.at[g], device(0, 0, 1)))
    for g, (p, n) in enumerate(FAR):
        take(core_in.at[pl.ds(p, n)], rc_r.at[g])
        mine = stage[pl.ds(p * 4 * SUB, n * 4 * SUB), :].reshape(n, NX, SUB, LANE)
        both = mine + core_in[pl.ds(p, n)].astype(F32)
        x_own[pl.ds(p, n)] = both[:, 0]
        for d in range(1, NX):
            x_out[d - 1, pl.ds(p, n)] = both[:, d].astype(BF16)
            sends.append(
                send(
                    x_out.at[d - 1, pl.ds(p, n)], x_in.at[NX - d - 1, pl.ds(p, n)],
                    rx_s.at[g, d - 1], rx_r.at[g, NX - d - 1], device(0, d, 0),
                )
            )
    for p in range(15):
        take(meta.at[p], am_r.at[p])
    for g, (p, n) in enumerate(FAR):
        for d in range(1, NX):
            take(x_in.at[d - 1, pl.ds(p, n)], rx_r.at[g, d - 1])
        for q in range(p, p + n):
            total = x_own[q]
            for d in range(1, NX):
                total += x_in[d - 1, q].astype(F32)
            factor = jnp.sum(jnp.where(lane == z, meta[q], 0.0), axis=1, keepdims=True)
            total *= factor
            if q == 15:
                x_own[q] = total
            else:
                k = K_OF[q]
                there = P_OF[NZ - k]
                z_out[q] = total.astype(BF16)
                sends.append(send(z_out.at[q], z_in.at[there], rz_s.at[q], rz_r.at[there], device(k, 0, 0)))
    total = x_own[15]
    for p in range(15):
        take(z_in.at[p], rz_r.at[p])
        total += z_in[p].astype(F32)
    out_ref[...] = total.astype(BF16)
    for copy in sends:
        copy.wait_send()


def shards(tokens, expert_ids, gates, gate_weight, up_weight, down_weight):
    hidden_dev, width = gate_weight.shape[1:]
    sems = pltpu.SemaphoreType.DMA
    vmem = pl.BlockSpec(memory_space=pltpu.VMEM)
    hbm = pl.BlockSpec(memory_space=pl.ANY)
    result = pl.pallas_call(
        kernel,
        name="routed_experts",
        out_shape=jax.ShapeDtypeStruct((SUB, LANE), BF16),
        in_specs=[vmem, vmem, vmem, hbm, hbm, hbm],
        out_specs=vmem,
        scratch_shapes=[
            pltpu.VMEM((hidden_dev, width), BF16),
            pltpu.VMEM((hidden_dev, width), BF16),
            pltpu.VMEM((hidden_dev, width), BF16),
            pltpu.VMEM((SUB, LANE), BF16),
            pltpu.VMEM((NC, NZ, NX, SUB, LANE), BF16),
            pltpu.VMEM((NZ, 1, LANE), F32),
            pltpu.VMEM((128 * SUB, LANE), F32),
            pltpu.VMEM((128, width), BF16),
            pltpu.VMEM((NZ, NX, SUB, LANE), BF16),
            pltpu.VMEM((NZ, NX, SUB, LANE), BF16),
            pltpu.VMEM((NX - 1, NZ, SUB, LANE), BF16),
            pltpu.VMEM((NX - 1, NZ, SUB, LANE), BF16),
            pltpu.VMEM((NZ, SUB, LANE), F32),
            pltpu.VMEM((NZ - 1, SUB, LANE), BF16),
            pltpu.VMEM((NZ - 1, SUB, LANE), BF16),
            sems((3,)),
            sems((15,)), sems((15,)), sems((15,)), sems((15,)),
            sems((9, 3)), sems((9, 3)), sems((9,)), sems((9,)),
            sems((9,)), sems((9,)), sems((9, 3)), sems((9, 3)),
            sems((15,)), sems((15,)),
        ],
        compiler_params=pltpu.CompilerParams(collective_id=0, has_side_effects=True),
    )(tokens, expert_ids, gates, gate_weight, up_weight, down_weight)
    return result.reshape(1, width)


def solution(mesh):
    return jax.shard_map(
        shards,
        mesh=mesh,
        in_specs=(
            P(("dp", "ep"), None),
            P(("dp", "ep"), None),
            P(("dp", "ep"), None),
            P("ep", None, None),
            P("ep", None, None),
            P("ep", None, None),
        ),
        out_specs=P(("dp", "ep"), None),
        check_vma=False,
    )
```

```python
import functools

import jax
import jax.numpy as jnp
from jax import lax
from jax.experimental import pallas as pl
from jax.experimental.pallas import tpu as pltpu
from jax.sharding import PartitionSpec as P

MESH = pl.DeviceIdType.MESH
F32 = jnp.float32
BF16 = jnp.bfloat16
NZ, NX, NC = 16, 4, 2
SUB, LANE = 32, 128

K_OF = [k for j in range(1, 8) for k in (j, NZ - j)] + [8, 0]
P_OF = {k: p for p, k in enumerate(K_OF)}
NEAR = [(15, 1)] + [(2 * j, 2) for j in range(7)] + [(14, 1)]
FAR = NEAR[::-1]
OUT_DIRECT = 2
BACK_DIRECT = 1
BACK_LATE = ([(14, 0)] + FAR)[BACK_DIRECT][0]
SLOTS = 15 - BACK_LATE
LEG = 3


def kernel(
    tok_hbm, ids_hbm, gate_hbm, wg_hbm, wu_hbm, wd_hbm, out_ref,
    tok_ref, ids_ref, gate_ref, wg, wu, wd, own, got, meta, stage, rows,
    core_out, core_in, x_out, x_in, late_out, late_in, x_own, z_out, z_in,
    w_sem, az_s, az_r, am_s, am_r, ax_s, ax_r, ac_s, ac_r, rc_s, rc_r, rx_s, rx_r, rl_s, rl_r, rz_s, rz_r,
):
    me = lax.axis_index("ep")
    core = lax.rem(me, NC)
    x = lax.rem(me // NC, NX)
    z = me // (NC * NX)

    def device(dz, dx, dc):
        pz = lax.rem(z + dz, NZ)
        px = lax.rem(x + dx, NX)
        pc = lax.rem(core + dc, NC)
        return {"ep": (pz * NX + px) * NC + pc}

    def send(src, dst, s_sem, r_sem, to):
        copy = pltpu.make_async_remote_copy(
            src_ref=src, dst_ref=dst, send_sem=s_sem, recv_sem=r_sem, device_id=to, device_id_type=MESH
        )
        copy.start()
        return copy

    plane = [(dx, dc) for dc in range(NC) for dx in range(NX)][1:]
    peers = [device(s * d % NZ, 0, 0) for d in range(1, LEG + 1) for s in (1, -1)] + [device(0, dx, dc) for dx, dc in plane]
    barrier = pltpu.get_barrier_semaphore()
    for peer in peers:
        pl.semaphore_signal(barrier, inc=1, device_id=peer, device_id_type=MESH)

    loads = []
    for n, (src, dst) in enumerate(
        (
            (tok_hbm, tok_ref), (ids_hbm, ids_ref), (gate_hbm, gate_ref),
            (wg_hbm.at[0], wg), (wu_hbm.at[0], wu), (wd_hbm.at[0], wd),
        )
    ):
        copy = pltpu.make_async_copy(src, dst, w_sem.at[n])
        copy.start()
        loads.append(copy)
    for copy in loads[:3]:
        copy.wait()

    lane = lax.broadcasted_iota(jnp.int32, (1, LANE), 1)
    row = tok_ref[...].astype(F32)
    for j in range(SUB):
        stage[j : j + 1, :] = row[:, j * LANE : (j + 1) * LANE]
    own_row = stage[0:SUB, :].astype(BF16)
    own[...] = own_row
    got[0, 15, 0] = own_row
    weight = jnp.zeros((1, LANE), F32)
    for k in range(ids_ref.shape[1]):
        weight += jnp.where(lane == ids_ref[:, k : k + 1], gate_ref[:, k : k + 1], 0.0)
    meta[15] = weight

    pl.semaphore_wait(barrier, len(peers))

    sends = []
    for d in range(LEG, 0, -1):
        for step in (d, NZ - d):
            p = P_OF[NZ - step]
            sends.append(send(own, got.at[0, p, 0], az_s.at[p], az_r.at[p], device(step, 0, 0)))

    def gates_along_z():
        for d in range(1, NZ):
            p = P_OF[NZ - d]
            sends.append(send(meta.at[15], meta.at[p], am_s.at[p], am_r.at[p], device(d, 0, 0)))

    def take(dst, r_sem):
        pltpu.make_async_copy(dst, dst, r_sem).wait()

    def rows_along_x(g):
        p, n = NEAR[g]
        if g not in (0, LEG):
            for q in range(p, p + n):
                take(got.at[0, q, 0], az_r.at[q])
        for dx, dc in plane if g > 8 - OUT_DIRECT else plane[: NX - 1]:
            px = (NX - dx) % NX
            sends.append(
                send(
                    got.at[0, pl.ds(p, n), 0], got.at[dc, pl.ds(p, n), px],
                    ax_s.at[g, dc, dx], ax_r.at[g, dc, px], device(0, dx, dc),
                )
            )

    def hand_on():
        below, above = P_OF[NZ - LEG], P_OF[LEG]
        take(got.at[0, below, 0], az_r.at[below])
        take(got.at[0, above, 0], az_r.at[above])
        for m in range(NZ // 2 - LEG, 0, -1):
            hops = [(below, m)] if LEG + m == NZ // 2 else [(below, m), (above, NZ - m)]
            for held, step in hops:
                p = P_OF[(K_OF[held] - step) % NZ]
                sends.append(send(got.at[0, held, 0], got.at[0, p, 0], az_s.at[p], az_r.at[p], device(step, 0, 0)))

    def rows_to_partner(g):
        p, n = NEAR[g]
        for d in range(1, NX):
            take(got.at[0, pl.ds(p, n), d], ax_r.at[g, 0, d])
        sends.append(send(got.at[0, pl.ds(p, n)], got.at[1, pl.ds(p, n)], ac_s.at[g], ac_r.at[g], device(0, 0, 1)))

    def unpack(side, unit):
        base = side * 64 + unit * 16
        stage[pl.ds(base * SUB, 16 * SUB), :] = (
            got[side, 4 * unit : 4 * unit + 4].astype(F32).reshape(16 * SUB, LANE)
        )
        for j in range(SUB):
            rows[pl.ds(base, 16), j * LANE : (j + 1) * LANE] = stage[
                pl.ds(base * SUB + j, 16, stride=SUB), :
            ].astype(BF16)

    def rows_from_partner(g):
        p, n = NEAR[g]
        take(got.at[1, pl.ds(p, n)], ac_r.at[g])

    def late_rows(g):
        p, n = NEAR[g]
        for dx, dc in plane:
            take(got.at[dc, pl.ds(p, n), dx], ax_r.at[g, dc, dx])

    rows_along_x(0)
    rows_along_x(1)
    rows_along_x(2)
    hand_on()
    rows_along_x(3)
    rows_to_partner(0)
    rows_to_partner(1)
    rows_along_x(4)
    rows_to_partner(2)
    rows_along_x(5)
    rows_to_partner(3)
    rows_along_x(6)
    rows_along_x(7)
    rows_along_x(8)
    gates_along_z()
    rows_to_partner(4)
    unpack(0, 0)
    rows_to_partner(5)
    unpack(0, 1)
    rows_to_partner(6)
    unpack(0, 2)
    rows_from_partner(1)
    rows_from_partner(2)
    unpack(1, 0)
    rows_from_partner(3)
    rows_from_partner(4)
    unpack(1, 1)
    if OUT_DIRECT < 2:
        rows_to_partner(7)
    rows_from_partner(5)
    rows_from_partner(6)
    unpack(1, 2)
    rows_from_partner(0)
    for g in range(9 - OUT_DIRECT, 9):
        late_rows(g)
    unpack(0, 3)
    if OUT_DIRECT < 2:
        rows_from_partner(7)
    if OUT_DIRECT < 1:
        rows_to_partner(8)
        rows_from_partner(8)
    unpack(1, 3)

    for copy in loads[3:]:
        copy.wait()
    contract = (((1,), (1,)), ((), ()))
    gate_act = lax.dot_general(rows[...], wg[...], contract, preferred_element_type=F32)
    up_act = lax.dot_general(rows[...], wu[...], contract, preferred_element_type=F32)
    hidden = (jax.nn.silu(gate_act) * up_act).astype(BF16)
    for n in range(16):
        value = jnp.dot(hidden, wd[:, n * 256 : (n + 1) * 256], preferred_element_type=F32)
        stage[pl.ds(2 * n, 128, stride=SUB), :] = value[:, :LANE]
        stage[pl.ds(2 * n + 1, 128, stride=SUB), :] = value[:, LANE:]

    for g, (p, n) in enumerate(FAR[:BACK_DIRECT]):
        for dx, dc in plane:
            px = (NX - dx) % NX
            for q in range(n):
                row = ((dc * NZ + p + q) * NX + dx) * SUB
                late_out[dc, dx, p - BACK_LATE + q] = stage[pl.ds(row, SUB), :].astype(BF16)
            sends.append(
                send(
                    late_out.at[dc, dx, pl.ds(p - BACK_LATE, n)], late_in.at[dc, px, pl.ds(p - BACK_LATE, n)],
                    rl_s.at[g, dc, dx], rl_r.at[g, dc, px], device(0, dx, dc),
                )
            )
    for g, (p, n) in enumerate(FAR):
        if g < BACK_DIRECT:
            continue
        core_out[pl.ds(p, n)] = (
            stage[pl.ds((64 + p * 4) * SUB, n * 4 * SUB), :].astype(BF16).reshape(n, NX, SUB, LANE)
        )
        sends.append(send(core_out.at[pl.ds(p, n)], core_in.at[pl.ds(p, n)], rc_s.at[g], rc_r.at[g], device(0, 0, 1)))
    for g, (p, n) in enumerate(FAR):
        if g < BACK_DIRECT:
            continue
        take(core_in.at[pl.ds(p, n)], rc_r.at[g])
        mine = stage[pl.ds(p * 4 * SUB, n * 4 * SUB), :].reshape(n, NX, SUB, LANE)
        both = mine + core_in[pl.ds(p, n)].astype(F32)
        x_own[pl.ds(p, n)] = both[:, 0]
        for d in range(1, NX):
            x_out[d - 1, pl.ds(p, n)] = both[:, d].astype(BF16)
            sends.append(
                send(
                    x_out.at[d - 1, pl.ds(p, n)], x_in.at[NX - d - 1, pl.ds(p, n)],
                    rx_s.at[g, d - 1], rx_r.at[g, NX - d - 1], device(0, d, 0),
                )
            )
    for p in range(15):
        take(meta.at[p], am_r.at[p])
    for g, (p, n) in enumerate(FAR):
        if g < BACK_DIRECT:
            for dx, dc in plane:
                take(late_in.at[dc, dx, pl.ds(p - BACK_LATE, n)], rl_r.at[g, dc, dx])
        else:
            for d in range(1, NX):
                take(x_in.at[d - 1, pl.ds(p, n)], rx_r.at[g, d - 1])
        for q in range(p, p + n):
            if g < BACK_DIRECT:
                total = stage[pl.ds(q * NX * SUB, SUB), :]
                for dx, dc in plane:
                    total += late_in[dc, dx, q - BACK_LATE].astype(F32)
            else:
                total = x_own[q]
                for d in range(1, NX):
                    total += x_in[d - 1, q].astype(F32)
            factor = jnp.sum(jnp.where(lane == z, meta[q], 0.0), axis=1, keepdims=True)
            total *= factor
            if q == 15:
                x_own[q] = total
            else:
                k = K_OF[q]
                there = P_OF[NZ - k]
                z_out[q] = total.astype(BF16)
                sends.append(send(z_out.at[q], z_in.at[there], rz_s.at[q], rz_r.at[there], device(k, 0, 0)))
    total = x_own[15]
    for p in range(15):
        take(z_in.at[p], rz_r.at[p])
        total += z_in[p].astype(F32)
    out_ref[...] = total.astype(BF16)
    for copy in sends:
        copy.wait_send()


def shards(tokens, expert_ids, gates, gate_weight, up_weight, down_weight):
    hidden_dev, width = gate_weight.shape[1:]
    sems = pltpu.SemaphoreType.DMA
    vmem = pl.BlockSpec(memory_space=pltpu.VMEM)
    hbm = pl.BlockSpec(memory_space=pl.ANY)
    result = pl.pallas_call(
        kernel,
        name="routed_experts",
        out_shape=pltpu.VMEM((SUB, LANE), BF16),
        in_specs=[hbm] * 6,
        out_specs=vmem,
        scratch_shapes=[
            pltpu.VMEM((1, width), BF16),
            pltpu.VMEM(expert_ids.shape, jnp.int32),
            pltpu.VMEM(gates.shape, F32),
            pltpu.VMEM((hidden_dev, width), BF16),
            pltpu.VMEM((hidden_dev, width), BF16),
            pltpu.VMEM((hidden_dev, width), BF16),
            pltpu.VMEM((SUB, LANE), BF16),
            pltpu.VMEM((NC, NZ, NX, SUB, LANE), BF16),
            pltpu.VMEM((NZ, 1, LANE), F32),
            pltpu.VMEM((128 * SUB, LANE), F32),
            pltpu.VMEM((128, width), BF16),
            pltpu.VMEM((NZ, NX, SUB, LANE), BF16),
            pltpu.VMEM((NZ, NX, SUB, LANE), BF16),
            pltpu.VMEM((NX - 1, NZ, SUB, LANE), BF16),
            pltpu.VMEM((NX - 1, NZ, SUB, LANE), BF16),
            pltpu.VMEM((NC, NX, SLOTS, SUB, LANE), BF16),
            pltpu.VMEM((NC, NX, SLOTS, SUB, LANE), BF16),
            pltpu.VMEM((NZ, SUB, LANE), F32),
            pltpu.VMEM((NZ - 1, SUB, LANE), BF16),
            pltpu.VMEM((NZ - 1, SUB, LANE), BF16),
            sems((6,)),
            sems((15,)), sems((15,)), sems((15,)), sems((15,)),
            sems((9, NC, NX)), sems((9, NC, NX)), sems((9,)), sems((9,)),
            sems((9,)), sems((9,)), sems((9, 3)), sems((9, 3)),
            sems((max(BACK_DIRECT, 1), NC, NX)), sems((max(BACK_DIRECT, 1), NC, NX)),
            sems((15,)), sems((15,)),
        ],
        compiler_params=pltpu.CompilerParams(collective_id=0, has_side_effects=True),
    )(tokens, expert_ids, gates, gate_weight, up_weight, down_weight)
    return result.reshape(1, width)


def solution(mesh):
    return jax.shard_map(
        shards,
        mesh=mesh,
        in_specs=(
            P(("dp", "ep"), None),
            P(("dp", "ep"), None),
            P(("dp", "ep"), None),
            P("ep", None, None),
            P("ep", None, None),
            P("ep", None, None),
        ),
        out_specs=P(("dp", "ep"), None),
        check_vma=False,
    )
```

```python
import functools

import jax
import jax.numpy as jnp
from jax import lax
from jax.experimental import pallas as pl
from jax.experimental.pallas import tpu as pltpu
from jax.sharding import PartitionSpec as P

MESH = pl.DeviceIdType.MESH
F32 = jnp.float32
BF16 = jnp.bfloat16
NZ, NX, NC = 16, 4, 2
SUB, LANE = 32, 128

K_OF = [k for j in range(1, 8) for k in (j, NZ - j)] + [8, 0]
P_OF = {k: p for p, k in enumerate(K_OF)}
NEAR = [(15, 1)] + [(2 * j, 2) for j in range(7)] + [(14, 1)]
FAR = NEAR[::-1]
OUT_DIRECT = 2
BACK_DIRECT = 1
BACK_LATE = ([(14, 0)] + FAR)[BACK_DIRECT][0]
SLOTS = 15 - BACK_LATE
LEG = 3


def kernel(
    tok_hbm, ids_hbm, gate_hbm, wg_hbm, wu_hbm, wd_hbm, out_ref,
    tok_ref, ids_ref, gate_ref, wg, wu, wd, own, got, meta, stage, rows,
    core_out, core_in, x_out, x_in, late_out, late_in, x_own, z_out, z_in,
    w_sem, az_s, az_r, am_s, am_r, ax_s, ax_r, ac_s, ac_r, rc_s, rc_r, rx_s, rx_r, rl_s, rl_r, rz_s, rz_r,
):
    me = lax.axis_index("ep")
    core = lax.rem(me, NC)
    x = lax.rem(me // NC, NX)
    z = me // (NC * NX)

    def device(dz, dx, dc):
        pz = lax.rem(z + dz, NZ)
        px = lax.rem(x + dx, NX)
        pc = lax.rem(core + dc, NC)
        return {"ep": (pz * NX + px) * NC + pc}

    def send(src, dst, s_sem, r_sem, to):
        copy = pltpu.make_async_remote_copy(
            src_ref=src, dst_ref=dst, send_sem=s_sem, recv_sem=r_sem, device_id=to, device_id_type=MESH
        )
        copy.start()
        return copy

    plane = [(dx, dc) for dc in range(NC) for dx in range(NX)][1:]
    peers = [device(s * d % NZ, 0, 0) for d in range(1, LEG + 1) for s in (1, -1)] + [device(0, dx, dc) for dx, dc in plane]
    barrier = pltpu.get_barrier_semaphore()
    for peer in peers:
        pl.semaphore_signal(barrier, inc=1, device_id=peer, device_id_type=MESH)

    loads = []
    for n, (src, dst) in enumerate(
        (
            (tok_hbm, tok_ref), (ids_hbm, ids_ref), (gate_hbm, gate_ref),
            (wg_hbm.at[0], wg), (wu_hbm.at[0], wu), (wd_hbm.at[0], wd),
        )
    ):
        copy = pltpu.make_async_copy(src, dst, w_sem.at[n])
        copy.start()
        loads.append(copy)
    for copy in loads[:3]:
        copy.wait()

    lane = lax.broadcasted_iota(jnp.int32, (1, LANE), 1)
    row = tok_ref[...].astype(F32)
    for j in range(SUB):
        stage[j : j + 1, :] = row[:, j * LANE : (j + 1) * LANE]
    own_row = stage[0:SUB, :].astype(BF16)
    own[...] = own_row
    got[0, 15, 0] = own_row
    weight = jnp.zeros((1, LANE), F32)
    for k in range(ids_ref.shape[1]):
        weight += jnp.where(lane == ids_ref[:, k : k + 1], gate_ref[:, k : k + 1], 0.0)
    meta[15] = weight

    pl.semaphore_wait(barrier, len(peers))

    sends = []
    for d in range(LEG, 0, -1):
        for step in (d, NZ - d):
            p = P_OF[NZ - step]
            sends.append(send(own, got.at[0, p, 0], az_s.at[p], az_r.at[p], device(step, 0, 0)))

    def gates_along_z():
        for d in range(1, NZ):
            p = P_OF[NZ - d]
            sends.append(send(meta.at[15], meta.at[p], am_s.at[p], am_r.at[p], device(d, 0, 0)))

    def take(dst, r_sem):
        pltpu.make_async_copy(dst, dst, r_sem).wait()

    def rows_along_x(g):
        p, n = NEAR[g]
        if g not in (0, LEG):
            for q in range(p, p + n):
                take(got.at[0, q, 0], az_r.at[q])
        for dx, dc in plane if g > 8 - OUT_DIRECT else plane[: NX - 1]:
            px = (NX - dx) % NX
            sends.append(
                send(
                    got.at[0, pl.ds(p, n), 0], got.at[dc, pl.ds(p, n), px],
                    ax_s.at[g, dc, dx], ax_r.at[g, dc, px], device(0, dx, dc),
                )
            )

    def hand_on():
        below, above = P_OF[NZ - LEG], P_OF[LEG]
        take(got.at[0, below, 0], az_r.at[below])
        take(got.at[0, above, 0], az_r.at[above])
        for m in range(NZ // 2 - LEG, 0, -1):
            hops = [(below, m)] if LEG + m == NZ // 2 else [(below, m), (above, NZ - m)]
            for held, step in hops:
                p = P_OF[(K_OF[held] - step) % NZ]
                sends.append(send(got.at[0, held, 0], got.at[0, p, 0], az_s.at[p], az_r.at[p], device(step, 0, 0)))

    def rows_to_partner(g):
        p, n = NEAR[g]
        for d in range(1, NX):
            take(got.at[0, pl.ds(p, n), d], ax_r.at[g, 0, d])
        sends.append(send(got.at[0, pl.ds(p, n)], got.at[1, pl.ds(p, n)], ac_s.at[g], ac_r.at[g], device(0, 0, 1)))

    def unpack(side, unit):
        base = side * 64 + unit * 16
        stage[pl.ds(base * SUB, 16 * SUB), :] = (
            got[side, 4 * unit : 4 * unit + 4].astype(F32).reshape(16 * SUB, LANE)
        )
        for j in range(SUB):
            rows[pl.ds(base, 16), j * LANE : (j + 1) * LANE] = stage[
                pl.ds(base * SUB + j, 16, stride=SUB), :
            ].astype(BF16)

    def rows_from_partner(g):
        p, n = NEAR[g]
        take(got.at[1, pl.ds(p, n)], ac_r.at[g])

    def late_rows(g):
        p, n = NEAR[g]
        for dx, dc in plane:
            take(got.at[dc, pl.ds(p, n), dx], ax_r.at[g, dc, dx])

    for g in range(LEG):
        rows_along_x(g)
    hand_on()
    for g in range(LEG, 9):
        rows_along_x(g)
    gates_along_z()
    for g in range(5):
        rows_to_partner(g)
    unpack(0, 0)
    rows_to_partner(5)
    unpack(0, 1)
    rows_to_partner(6)
    unpack(0, 2)
    rows_from_partner(1)
    rows_from_partner(2)
    unpack(1, 0)
    rows_from_partner(3)
    rows_from_partner(4)
    unpack(1, 1)
    if OUT_DIRECT < 2:
        rows_to_partner(7)
    rows_from_partner(5)
    rows_from_partner(6)
    unpack(1, 2)
    rows_from_partner(0)
    for g in range(9 - OUT_DIRECT, 9):
        late_rows(g)
    unpack(0, 3)
    if OUT_DIRECT < 2:
        rows_from_partner(7)
    if OUT_DIRECT < 1:
        rows_to_partner(8)
        rows_from_partner(8)
    unpack(1, 3)

    for copy in loads[3:]:
        copy.wait()
    contract = (((1,), (1,)), ((), ()))
    gate_act = lax.dot_general(rows[...], wg[...], contract, preferred_element_type=F32)
    up_act = lax.dot_general(rows[...], wu[...], contract, preferred_element_type=F32)
    hidden = (jax.nn.silu(gate_act) * up_act).astype(BF16)

    def down(blocks):
        size = blocks[0][1] - blocks[0][0]
        some = jnp.concatenate([hidden[first:last] for first, last in blocks], axis=0)
        for n in range(16):
            value = jnp.dot(some, wd[:, n * 256 : (n + 1) * 256], preferred_element_type=F32)
            for b, (first, _) in enumerate(blocks):
                part = value[b * size : (b + 1) * size]
                stage[pl.ds(first * SUB + 2 * n, size, stride=SUB), :] = part[:, :LANE]
                stage[pl.ds(first * SUB + 2 * n + 1, size, stride=SUB), :] = part[:, LANE:]

    down([(48, 64), (112, 128)])
    for g, (p, n) in enumerate(FAR[:BACK_DIRECT]):
        for dx, dc in plane:
            px = (NX - dx) % NX
            for q in range(n):
                row = ((dc * NZ + p + q) * NX + dx) * SUB
                late_out[dc, dx, p - BACK_LATE + q] = stage[pl.ds(row, SUB), :].astype(BF16)
            sends.append(
                send(
                    late_out.at[dc, dx, pl.ds(p - BACK_LATE, n)], late_in.at[dc, px, pl.ds(p - BACK_LATE, n)],
                    rl_s.at[g, dc, dx], rl_r.at[g, dc, px], device(0, dx, dc),
                )
            )
    for g, (p, n) in enumerate(FAR):
        if g == 2:
            down([(0, 48), (64, 112)])
        if g < BACK_DIRECT:
            continue
        core_out[pl.ds(p, n)] = (
            stage[pl.ds((64 + p * 4) * SUB, n * 4 * SUB), :].astype(BF16).reshape(n, NX, SUB, LANE)
        )
        sends.append(send(core_out.at[pl.ds(p, n)], core_in.at[pl.ds(p, n)], rc_s.at[g], rc_r.at[g], device(0, 0, 1)))
    for g, (p, n) in enumerate(FAR):
        if g < BACK_DIRECT:
            continue
        take(core_in.at[pl.ds(p, n)], rc_r.at[g])
        mine = stage[pl.ds(p * 4 * SUB, n * 4 * SUB), :].reshape(n, NX, SUB, LANE)
        both = mine + core_in[pl.ds(p, n)].astype(F32)
        x_own[pl.ds(p, n)] = both[:, 0]
        for d in range(1, NX):
            x_out[d - 1, pl.ds(p, n)] = both[:, d].astype(BF16)
            sends.append(
                send(
                    x_out.at[d - 1, pl.ds(p, n)], x_in.at[NX - d - 1, pl.ds(p, n)],
                    rx_s.at[g, d - 1], rx_r.at[g, NX - d - 1], device(0, d, 0),
                )
            )
    for p in range(15):
        take(meta.at[p], am_r.at[p])
    for g, (p, n) in enumerate(FAR):
        if g < BACK_DIRECT:
            for dx, dc in plane:
                take(late_in.at[dc, dx, pl.ds(p - BACK_LATE, n)], rl_r.at[g, dc, dx])
        else:
            for d in range(1, NX):
                take(x_in.at[d - 1, pl.ds(p, n)], rx_r.at[g, d - 1])
        for q in range(p, p + n):
            if g < BACK_DIRECT:
                total = stage[pl.ds(q * NX * SUB, SUB), :]
                for dx, dc in plane:
                    total += late_in[dc, dx, q - BACK_LATE].astype(F32)
            else:
                total = x_own[q]
                for d in range(1, NX):
                    total += x_in[d - 1, q].astype(F32)
            factor = jnp.sum(jnp.where(lane == z, meta[q], 0.0), axis=1, keepdims=True)
            total *= factor
            if q == 15:
                x_own[q] = total
            else:
                k = K_OF[q]
                there = P_OF[NZ - k]
                z_out[q] = total.astype(BF16)
                sends.append(send(z_out.at[q], z_in.at[there], rz_s.at[q], rz_r.at[there], device(k, 0, 0)))
    total = x_own[15]
    for p in range(15):
        take(z_in.at[p], rz_r.at[p])
        total += z_in[p].astype(F32)
    out_ref[...] = total.astype(BF16)
    for copy in sends:
        copy.wait_send()


def shards(tokens, expert_ids, gates, gate_weight, up_weight, down_weight):
    hidden_dev, width = gate_weight.shape[1:]
    sems = pltpu.SemaphoreType.DMA
    vmem = pl.BlockSpec(memory_space=pltpu.VMEM)
    hbm = pl.BlockSpec(memory_space=pl.ANY)
    result = pl.pallas_call(
        kernel,
        name="routed_experts",
        out_shape=pltpu.VMEM((SUB, LANE), BF16),
        in_specs=[hbm] * 6,
        out_specs=vmem,
        scratch_shapes=[
            pltpu.VMEM((1, width), BF16),
            pltpu.VMEM(expert_ids.shape, jnp.int32),
            pltpu.VMEM(gates.shape, F32),
            pltpu.VMEM((hidden_dev, width), BF16),
            pltpu.VMEM((hidden_dev, width), BF16),
            pltpu.VMEM((hidden_dev, width), BF16),
            pltpu.VMEM((SUB, LANE), BF16),
            pltpu.VMEM((NC, NZ, NX, SUB, LANE), BF16),
            pltpu.VMEM((NZ, 1, LANE), F32),
            pltpu.VMEM((128 * SUB, LANE), F32),
            pltpu.VMEM((128, width), BF16),
            pltpu.VMEM((NZ, NX, SUB, LANE), BF16),
            pltpu.VMEM((NZ, NX, SUB, LANE), BF16),
            pltpu.VMEM((NX - 1, NZ, SUB, LANE), BF16),
            pltpu.VMEM((NX - 1, NZ, SUB, LANE), BF16),
            pltpu.VMEM((NC, NX, SLOTS, SUB, LANE), BF16),
            pltpu.VMEM((NC, NX, SLOTS, SUB, LANE), BF16),
            pltpu.VMEM((NZ, SUB, LANE), F32),
            pltpu.VMEM((NZ - 1, SUB, LANE), BF16),
            pltpu.VMEM((NZ - 1, SUB, LANE), BF16),
            sems((6,)),
            sems((15,)), sems((15,)), sems((15,)), sems((15,)),
            sems((9, NC, NX)), sems((9, NC, NX)), sems((9,)), sems((9,)),
            sems((9,)), sems((9,)), sems((9, 3)), sems((9, 3)),
            sems((max(BACK_DIRECT, 1), NC, NX)), sems((max(BACK_DIRECT, 1), NC, NX)),
            sems((15,)), sems((15,)),
        ],
        compiler_params=pltpu.CompilerParams(collective_id=0, has_side_effects=True),
    )(tokens, expert_ids, gates, gate_weight, up_weight, down_weight)
    return result.reshape(1, width)


def solution(mesh):
    return jax.shard_map(
        shards,
        mesh=mesh,
        in_specs=(
            P(("dp", "ep"), None),
            P(("dp", "ep"), None),
            P(("dp", "ep"), None),
            P("ep", None, None),
            P("ep", None, None),
            P("ep", None, None),
        ),
        out_specs=P(("dp", "ep"), None),
        check_vma=False,
    )
```

```python
import functools

import jax
import jax.numpy as jnp
from jax import lax
from jax.experimental import pallas as pl
from jax.experimental.pallas import tpu as pltpu
from jax.sharding import PartitionSpec as P

MESH = pl.DeviceIdType.MESH
F32 = jnp.float32
BF16 = jnp.bfloat16
NZ, NX, NC = 16, 4, 2
SUB, LANE = 32, 128

K_OF = [k for j in range(1, 8) for k in (j, NZ - j)] + [8, 0]
P_OF = {k: p for p, k in enumerate(K_OF)}
NEAR = [(15, 1)] + [(2 * j, 2) for j in range(7)] + [(14, 1)]
FAR = NEAR[::-1]
OUT_DIRECT = 2
BACK_DIRECT = 1
BACK_LATE = ([(14, 0)] + FAR)[BACK_DIRECT][0]
SLOTS = 15 - BACK_LATE
LEG = 3


def kernel(
    tok_hbm, ids_hbm, gate_hbm, wg_hbm, wu_hbm, wd_hbm, out_ref,
    tok_ref, ids_ref, gate_ref, wg, wu, wd, own, got, meta, stage, rows,
    core_out, core_in, x_out, x_in, late_out, late_in, x_own, z_out, z_in,
    w_sem, az_s, az_r, am_s, am_r, ax_s, ax_r, ac_s, ac_r, rc_s, rc_r, rx_s, rx_r, rl_s, rl_r, rz_s, rz_r,
):
    me = lax.axis_index("ep")
    core = lax.rem(me, NC)
    x = lax.rem(me // NC, NX)
    z = me // (NC * NX)

    def device(dz, dx, dc):
        pz = lax.rem(z + dz, NZ)
        px = lax.rem(x + dx, NX)
        pc = lax.rem(core + dc, NC)
        return {"ep": (pz * NX + px) * NC + pc}

    def send(src, dst, s_sem, r_sem, to):
        copy = pltpu.make_async_remote_copy(
            src_ref=src, dst_ref=dst, send_sem=s_sem, recv_sem=r_sem, device_id=to, device_id_type=MESH
        )
        copy.start()
        return copy

    plane = [(dx, dc) for dc in range(NC) for dx in range(NX)][1:]
    late_order = [(2, 1), (2, 0), (1, 1), (3, 1), (1, 0), (3, 0), (0, 1)]
    peers = [device(s * d % NZ, 0, 0) for d in range(1, LEG + 1) for s in (1, -1)] + [device(0, dx, dc) for dx, dc in plane]
    barrier = pltpu.get_barrier_semaphore()
    for peer in peers:
        pl.semaphore_signal(barrier, inc=1, device_id=peer, device_id_type=MESH)

    loads = []
    for n, (src, dst) in enumerate(
        (
            (tok_hbm, tok_ref), (ids_hbm, ids_ref), (gate_hbm, gate_ref),
            (wg_hbm.at[0], wg), (wu_hbm.at[0], wu), (wd_hbm.at[0], wd),
        )
    ):
        copy = pltpu.make_async_copy(src, dst, w_sem.at[n])
        copy.start()
        loads.append(copy)
    for copy in loads[:3]:
        copy.wait()

    lane = lax.broadcasted_iota(jnp.int32, (1, LANE), 1)
    row = tok_ref[...].astype(F32)
    for j in range(SUB):
        stage[j : j + 1, :] = row[:, j * LANE : (j + 1) * LANE]
    own_row = stage[0:SUB, :].astype(BF16)
    own[...] = own_row
    got[0, 15, 0] = own_row
    weight = jnp.zeros((1, LANE), F32)
    for k in range(ids_ref.shape[1]):
        weight += jnp.where(lane == ids_ref[:, k : k + 1], gate_ref[:, k : k + 1], 0.0)
    meta[15] = weight

    pl.semaphore_wait(barrier, len(peers))

    sends = []
    for d in range(LEG, 0, -1):
        for step in (d, NZ - d):
            p = P_OF[NZ - step]
            sends.append(send(own, got.at[0, p, 0], az_s.at[p], az_r.at[p], device(step, 0, 0)))

    def gates_along_z():
        for d in range(1, NZ):
            p = P_OF[NZ - d]
            sends.append(send(meta.at[15], meta.at[p], am_s.at[p], am_r.at[p], device(d, 0, 0)))

    def take(dst, r_sem):
        pltpu.make_async_copy(dst, dst, r_sem).wait()

    def rows_along_x(g):
        p, n = NEAR[g]
        if g not in (0, LEG):
            for q in range(p, p + n):
                take(got.at[0, q, 0], az_r.at[q])
        for dx, dc in late_order if g > 8 - OUT_DIRECT else ((2, 0), (1, 0), (3, 0)):
            px = (NX - dx) % NX
            sends.append(
                send(
                    got.at[0, pl.ds(p, n), 0], got.at[dc, pl.ds(p, n), px],
                    ax_s.at[g, dc, dx], ax_r.at[g, dc, px], device(0, dx, dc),
                )
            )

    def hand_on():
        below, above = P_OF[NZ - LEG], P_OF[LEG]
        take(got.at[0, below, 0], az_r.at[below])
        take(got.at[0, above, 0], az_r.at[above])
        for m in range(NZ // 2 - LEG, 0, -1):
            hops = [(below, m)] if LEG + m == NZ // 2 else [(below, m), (above, NZ - m)]
            for held, step in hops:
                p = P_OF[(K_OF[held] - step) % NZ]
                sends.append(send(got.at[0, held, 0], got.at[0, p, 0], az_s.at[p], az_r.at[p], device(step, 0, 0)))

    def rows_to_partner(g):
        p, n = NEAR[g]
        for d in range(1, NX):
            take(got.at[0, pl.ds(p, n), d], ax_r.at[g, 0, d])
        sends.append(send(got.at[0, pl.ds(p, n)], got.at[1, pl.ds(p, n)], ac_s.at[g], ac_r.at[g], device(0, 0, 1)))

    def unpack(side, unit):
        base = side * 64 + unit * 16
        stage[pl.ds(base * SUB, 16 * SUB), :] = (
            got[side, 4 * unit : 4 * unit + 4].astype(F32).reshape(16 * SUB, LANE)
        )
        for j in range(SUB):
            rows[pl.ds(base, 16), j * LANE : (j + 1) * LANE] = stage[
                pl.ds(base * SUB + j, 16, stride=SUB), :
            ].astype(BF16)

    def rows_from_partner(g):
        p, n = NEAR[g]
        take(got.at[1, pl.ds(p, n)], ac_r.at[g])

    def late_rows(g):
        p, n = NEAR[g]
        for dx, dc in plane:
            take(got.at[dc, pl.ds(p, n), dx], ax_r.at[g, dc, dx])

    for g in range(LEG):
        rows_along_x(g)
    hand_on()
    for g in range(LEG, 9):
        rows_along_x(g)
    gates_along_z()
    for g in range(5):
        rows_to_partner(g)
    unpack(0, 0)
    rows_to_partner(5)
    unpack(0, 1)
    rows_to_partner(6)
    unpack(0, 2)
    rows_from_partner(1)
    rows_from_partner(2)
    unpack(1, 0)
    rows_from_partner(3)
    rows_from_partner(4)
    unpack(1, 1)
    if OUT_DIRECT < 2:
        rows_to_partner(7)
    rows_from_partner(5)
    rows_from_partner(6)
    unpack(1, 2)
    rows_from_partner(0)
    for g in range(9 - OUT_DIRECT, 9):
        late_rows(g)
    unpack(0, 3)
    if OUT_DIRECT < 2:
        rows_from_partner(7)
    if OUT_DIRECT < 1:
        rows_to_partner(8)
        rows_from_partner(8)
    unpack(1, 3)

    for copy in loads[3:]:
        copy.wait()
    contract = (((1,), (1,)), ((), ()))
    gate_act = lax.dot_general(rows[...], wg[...], contract, preferred_element_type=F32)
    up_act = lax.dot_general(rows[...], wu[...], contract, preferred_element_type=F32)
    hidden = (jax.nn.silu(gate_act) * up_act).astype(BF16)

    def down(blocks):
        size = blocks[0][1] - blocks[0][0]
        some = jnp.concatenate([hidden[first:last] for first, last in blocks], axis=0)
        for n in range(16):
            value = jnp.dot(some, wd[:, n * 256 : (n + 1) * 256], preferred_element_type=F32)
            for b, (first, _) in enumerate(blocks):
                part = value[b * size : (b + 1) * size]
                stage[pl.ds(first * SUB + 2 * n, size, stride=SUB), :] = part[:, :LANE]
                stage[pl.ds(first * SUB + 2 * n + 1, size, stride=SUB), :] = part[:, LANE:]

    down([(48, 64), (112, 128)])
    for g, (p, n) in enumerate(FAR[:BACK_DIRECT]):
        for dx, dc in late_order:
            px = (NX - dx) % NX
            for q in range(n):
                row = ((dc * NZ + p + q) * NX + dx) * SUB
                late_out[dc, dx, p - BACK_LATE + q] = stage[pl.ds(row, SUB), :].astype(BF16)
            sends.append(
                send(
                    late_out.at[dc, dx, pl.ds(p - BACK_LATE, n)], late_in.at[dc, px, pl.ds(p - BACK_LATE, n)],
                    rl_s.at[g, dc, dx], rl_r.at[g, dc, px], device(0, dx, dc),
                )
            )
    for g, (p, n) in enumerate(FAR):
        if g == 2:
            down([(0, 48), (64, 112)])
        if g < BACK_DIRECT:
            continue
        core_out[pl.ds(p, n)] = (
            stage[pl.ds((64 + p * 4) * SUB, n * 4 * SUB), :].astype(BF16).reshape(n, NX, SUB, LANE)
        )
        sends.append(send(core_out.at[pl.ds(p, n)], core_in.at[pl.ds(p, n)], rc_s.at[g], rc_r.at[g], device(0, 0, 1)))
    for g, (p, n) in enumerate(FAR):
        if g < BACK_DIRECT:
            continue
        take(core_in.at[pl.ds(p, n)], rc_r.at[g])
        mine = stage[pl.ds(p * 4 * SUB, n * 4 * SUB), :].reshape(n, NX, SUB, LANE)
        both = mine + core_in[pl.ds(p, n)].astype(F32)
        x_own[pl.ds(p, n)] = both[:, 0]
        for d in (2, 1, 3):
            x_out[d - 1, pl.ds(p, n)] = both[:, d].astype(BF16)
            sends.append(
                send(
                    x_out.at[d - 1, pl.ds(p, n)], x_in.at[NX - d - 1, pl.ds(p, n)],
                    rx_s.at[g, d - 1], rx_r.at[g, NX - d - 1], device(0, d, 0),
                )
            )
    for p in range(15):
        take(meta.at[p], am_r.at[p])
    for g, (p, n) in enumerate(FAR):
        if g < BACK_DIRECT:
            for dx, dc in plane:
                take(late_in.at[dc, dx, pl.ds(p - BACK_LATE, n)], rl_r.at[g, dc, dx])
        else:
            for d in range(1, NX):
                take(x_in.at[d - 1, pl.ds(p, n)], rx_r.at[g, d - 1])
        for q in range(p, p + n):
            if g < BACK_DIRECT:
                total = stage[pl.ds(q * NX * SUB, SUB), :]
                for dx, dc in plane:
                    total += late_in[dc, dx, q - BACK_LATE].astype(F32)
            else:
                total = x_own[q]
                for d in range(1, NX):
                    total += x_in[d - 1, q].astype(F32)
            factor = jnp.sum(jnp.where(lane == z, meta[q], 0.0), axis=1, keepdims=True)
            total *= factor
            if q == 15:
                x_own[q] = total
            else:
                k = K_OF[q]
                there = P_OF[NZ - k]
                z_out[q] = total.astype(BF16)
                sends.append(send(z_out.at[q], z_in.at[there], rz_s.at[q], rz_r.at[there], device(k, 0, 0)))
    for copy in sends[:-15]:
        copy.wait_send()
    total = x_own[15]
    for p in range(15):
        take(z_in.at[p], rz_r.at[p])
        total += z_in[p].astype(F32)
    out_ref[...] = total.astype(BF16)
    for copy in sends[-15:]:
        copy.wait_send()


def shards(tokens, expert_ids, gates, gate_weight, up_weight, down_weight):
    hidden_dev, width = gate_weight.shape[1:]
    sems = pltpu.SemaphoreType.DMA
    vmem = pl.BlockSpec(memory_space=pltpu.VMEM)
    hbm = pl.BlockSpec(memory_space=pl.ANY)
    result = pl.pallas_call(
        kernel,
        name="routed_experts",
        out_shape=pltpu.VMEM((SUB, LANE), BF16),
        in_specs=[hbm] * 6,
        out_specs=vmem,
        scratch_shapes=[
            pltpu.VMEM((1, width), BF16),
            pltpu.VMEM(expert_ids.shape, jnp.int32),
            pltpu.VMEM(gates.shape, F32),
            pltpu.VMEM((hidden_dev, width), BF16),
            pltpu.VMEM((hidden_dev, width), BF16),
            pltpu.VMEM((hidden_dev, width), BF16),
            pltpu.VMEM((SUB, LANE), BF16),
            pltpu.VMEM((NC, NZ, NX, SUB, LANE), BF16),
            pltpu.VMEM((NZ, 1, LANE), F32),
            pltpu.VMEM((128 * SUB, LANE), F32),
            pltpu.VMEM((128, width), BF16),
            pltpu.VMEM((NZ, NX, SUB, LANE), BF16),
            pltpu.VMEM((NZ, NX, SUB, LANE), BF16),
            pltpu.VMEM((NX - 1, NZ, SUB, LANE), BF16),
            pltpu.VMEM((NX - 1, NZ, SUB, LANE), BF16),
            pltpu.VMEM((NC, NX, SLOTS, SUB, LANE), BF16),
            pltpu.VMEM((NC, NX, SLOTS, SUB, LANE), BF16),
            pltpu.VMEM((NZ, SUB, LANE), F32),
            pltpu.VMEM((NZ - 1, SUB, LANE), BF16),
            pltpu.VMEM((NZ - 1, SUB, LANE), BF16),
            sems((6,)),
            sems((15,)), sems((15,)), sems((15,)), sems((15,)),
            sems((9, NC, NX)), sems((9, NC, NX)), sems((9,)), sems((9,)),
            sems((9,)), sems((9,)), sems((9, 3)), sems((9, 3)),
            sems((max(BACK_DIRECT, 1), NC, NX)), sems((max(BACK_DIRECT, 1), NC, NX)),
            sems((15,)), sems((15,)),
        ],
        compiler_params=pltpu.CompilerParams(collective_id=0, has_side_effects=True),
    )(tokens, expert_ids, gates, gate_weight, up_weight, down_weight)
    return result.reshape(1, width)


def solution(mesh):
    return jax.shard_map(
        shards,
        mesh=mesh,
        in_specs=(
            P(("dp", "ep"), None),
            P(("dp", "ep"), None),
            P(("dp", "ep"), None),
            P("ep", None, None),
            P("ep", None, None),
            P("ep", None, None),
        ),
        out_specs=P(("dp", "ep"), None),
        check_vma=False,
    )
```

```python
import functools

import jax
import jax.numpy as jnp
from jax import lax
from jax.experimental import pallas as pl
from jax.experimental.pallas import tpu as pltpu
from jax.sharding import PartitionSpec as P

MESH = pl.DeviceIdType.MESH
F32 = jnp.float32
BF16 = jnp.bfloat16
NZ, NX, NC = 16, 4, 2
SUB, LANE = 32, 128

K_OF = [k for j in range(1, 8) for k in (j, NZ - j)] + [8, 0]
P_OF = {k: p for p, k in enumerate(K_OF)}
NEAR = [(15, 1)] + [(2 * j, 2) for j in range(7)] + [(14, 1)]
FAR = NEAR[::-1]
OUT_DIRECT = 2
BACK_DIRECT = 1
BACK_LATE = ([(14, 0)] + FAR)[BACK_DIRECT][0]
SLOTS = 15 - BACK_LATE
LEG = 3


def kernel(
    tok_hbm, ids_hbm, gate_hbm, wg_hbm, wu_hbm, wd_hbm, out_ref,
    tok_ref, ids_ref, gate_ref, wg, wu, wd, own, got, meta, stage, rows,
    core_out, core_in, x_out, x_in, late_out, late_in, x_own, z_out, z_in,
    w_sem, az_s, az_r, am_s, am_r, ax_s, ax_r, ac_s, ac_r, rc_s, rc_r, rx_s, rx_r, rl_s, rl_r, rz_s, rz_r,
):
    me = lax.axis_index("ep")
    core = lax.rem(me, NC)
    x = lax.rem(me // NC, NX)
    z = me // (NC * NX)

    def device(dz, dx, dc):
        pz = lax.rem(z + dz, NZ)
        px = lax.rem(x + dx, NX)
        pc = lax.rem(core + dc, NC)
        return {"ep": (pz * NX + px) * NC + pc}

    def send(src, dst, s_sem, r_sem, to):
        copy = pltpu.make_async_remote_copy(
            src_ref=src, dst_ref=dst, send_sem=s_sem, recv_sem=r_sem, device_id=to, device_id_type=MESH
        )
        copy.start()
        return copy

    plane = [(dx, dc) for dc in range(NC) for dx in range(NX)][1:]
    late_order = [(2, 1), (2, 0), (1, 1), (3, 1), (1, 0), (3, 0), (0, 1)]
    peers = [device(s * d % NZ, 0, 0) for d in range(1, LEG + 1) for s in (1, -1)] + [device(0, dx, dc) for dx, dc in plane]
    barrier = pltpu.get_barrier_semaphore()
    for peer in peers:
        pl.semaphore_signal(barrier, inc=1, device_id=peer, device_id_type=MESH)

    loads = []
    for n, (src, dst) in enumerate(
        (
            (tok_hbm, tok_ref), (ids_hbm, ids_ref), (gate_hbm, gate_ref),
            (wg_hbm.at[0], wg), (wu_hbm.at[0], wu), (wd_hbm.at[0], wd),
        )
    ):
        copy = pltpu.make_async_copy(src, dst, w_sem.at[n])
        copy.start()
        loads.append(copy)
    for copy in loads[:3]:
        copy.wait()

    lane = lax.broadcasted_iota(jnp.int32, (1, LANE), 1)
    row = tok_ref[...].astype(F32)
    for j in range(SUB):
        stage[j : j + 1, :] = row[:, j * LANE : (j + 1) * LANE]
    own_row = stage[0:SUB, :].astype(BF16)
    own[...] = own_row
    got[0, 15, 0] = own_row
    weight = jnp.zeros((1, LANE), F32)
    for k in range(ids_ref.shape[1]):
        weight += jnp.where(lane == ids_ref[:, k : k + 1], gate_ref[:, k : k + 1], 0.0)
    meta[15] = weight

    pl.semaphore_wait(barrier, len(peers))

    sends = []
    for d in range(LEG, 0, -1):
        for step in (d, NZ - d):
            p = P_OF[NZ - step]
            sends.append(send(own, got.at[0, p, 0], az_s.at[p], az_r.at[p], device(step, 0, 0)))

    def gates_along_z():
        for d in range(1, NZ):
            p = P_OF[NZ - d]
            sends.append(send(meta.at[15], meta.at[p], am_s.at[p], am_r.at[p], device(d, 0, 0)))

    def take(dst, r_sem):
        pltpu.make_async_copy(dst, dst, r_sem).wait()

    def rows_along_x(g):
        p, n = NEAR[g]
        if g not in (0, LEG):
            for q in range(p, p + n):
                take(got.at[0, q, 0], az_r.at[q])
        for dx, dc in late_order if g > 8 - OUT_DIRECT else ((2, 0), (1, 0), (3, 0)):
            px = (NX - dx) % NX
            sends.append(
                send(
                    got.at[0, pl.ds(p, n), 0], got.at[dc, pl.ds(p, n), px],
                    ax_s.at[g, dc, dx], ax_r.at[g, dc, px], device(0, dx, dc),
                )
            )

    def hand_on():
        below, above = P_OF[NZ - LEG], P_OF[LEG]
        take(got.at[0, below, 0], az_r.at[below])
        take(got.at[0, above, 0], az_r.at[above])
        for m in range(NZ // 2 - LEG, 0, -1):
            hops = [(below, m)] if LEG + m == NZ // 2 else [(below, m), (above, NZ - m)]
            for held, step in hops:
                p = P_OF[(K_OF[held] - step) % NZ]
                sends.append(send(got.at[0, held, 0], got.at[0, p, 0], az_s.at[p], az_r.at[p], device(step, 0, 0)))

    def rows_to_partner(g):
        p, n = NEAR[g]
        for d in range(1, NX):
            take(got.at[0, pl.ds(p, n), d], ax_r.at[g, 0, d])
        sends.append(send(got.at[0, pl.ds(p, n)], got.at[1, pl.ds(p, n)], ac_s.at[g], ac_r.at[g], device(0, 0, 1)))

    def unpack(side, unit):
        base = side * 64 + unit * 16
        stage[pl.ds(base * SUB, 16 * SUB), :] = (
            got[side, 4 * unit : 4 * unit + 4].astype(F32).reshape(16 * SUB, LANE)
        )
        for j in range(SUB):
            rows[pl.ds(base, 16), j * LANE : (j + 1) * LANE] = stage[
                pl.ds(base * SUB + j, 16, stride=SUB), :
            ].astype(BF16)

    def rows_from_partner(g):
        p, n = NEAR[g]
        take(got.at[1, pl.ds(p, n)], ac_r.at[g])

    def late_rows(g):
        p, n = NEAR[g]
        for dx, dc in plane:
            take(got.at[dc, pl.ds(p, n), dx], ax_r.at[g, dc, dx])

    for g in range(LEG):
        rows_along_x(g)
    hand_on()
    for g in range(LEG, 9):
        rows_along_x(g)
    gates_along_z()
    for g in range(5):
        rows_to_partner(g)
    unpack(0, 0)
    rows_to_partner(5)
    unpack(0, 1)
    rows_to_partner(6)
    unpack(0, 2)
    rows_from_partner(1)
    rows_from_partner(2)
    unpack(1, 0)
    rows_from_partner(3)
    rows_from_partner(4)
    unpack(1, 1)
    if OUT_DIRECT < 2:
        rows_to_partner(7)
    rows_from_partner(5)
    rows_from_partner(6)
    unpack(1, 2)
    rows_from_partner(0)
    for g in range(9 - OUT_DIRECT, 9):
        late_rows(g)
    unpack(0, 3)
    if OUT_DIRECT < 2:
        rows_from_partner(7)
    if OUT_DIRECT < 1:
        rows_to_partner(8)
        rows_from_partner(8)
    unpack(1, 3)

    for copy in loads[3:]:
        copy.wait()
    contract = (((1,), (1,)), ((), ()))
    gate_act = lax.dot_general(rows[...], wg[...], contract, preferred_element_type=F32)
    up_act = lax.dot_general(rows[...], wu[...], contract, preferred_element_type=F32)
    hidden = (jax.nn.silu(gate_act) * up_act).astype(BF16)

    def down(blocks):
        size = blocks[0][1] - blocks[0][0]
        some = jnp.concatenate([hidden[first:last] for first, last in blocks], axis=0)
        for n in range(16):
            value = jnp.dot(some, wd[:, n * 256 : (n + 1) * 256], preferred_element_type=F32)
            for b, (first, _) in enumerate(blocks):
                part = value[b * size : (b + 1) * size]
                stage[pl.ds(first * SUB + 2 * n, size, stride=SUB), :] = part[:, :LANE]
                stage[pl.ds(first * SUB + 2 * n + 1, size, stride=SUB), :] = part[:, LANE:]

    down([(48, 64), (112, 128)])
    for g, (p, n) in enumerate(FAR[:BACK_DIRECT]):
        for dx, dc in late_order:
            px = (NX - dx) % NX
            for q in range(n):
                row = ((dc * NZ + p + q) * NX + dx) * SUB
                late_out[dc, dx, p - BACK_LATE + q] = stage[pl.ds(row, SUB), :].astype(BF16)
            sends.append(
                send(
                    late_out.at[dc, dx, pl.ds(p - BACK_LATE, n)], late_in.at[dc, px, pl.ds(p - BACK_LATE, n)],
                    rl_s.at[g, dc, dx], rl_r.at[g, dc, px], device(0, dx, dc),
                )
            )
    for g, (p, n) in enumerate(FAR):
        if g == 2:
            down([(0, 48), (64, 112)])
        if g < BACK_DIRECT:
            continue
        core_out[pl.ds(p, n)] = (
            stage[pl.ds((64 + p * 4) * SUB, n * 4 * SUB), :].astype(BF16).reshape(n, NX, SUB, LANE)
        )
        sends.append(send(core_out.at[pl.ds(p, n)], core_in.at[pl.ds(p, n)], rc_s.at[g], rc_r.at[g], device(0, 0, 1)))
    for g, (p, n) in enumerate(FAR):
        if g < BACK_DIRECT:
            continue
        take(core_in.at[pl.ds(p, n)], rc_r.at[g])
        mine = stage[pl.ds(p * 4 * SUB, n * 4 * SUB), :].reshape(n, NX, SUB, LANE)
        both = mine + core_in[pl.ds(p, n)].astype(F32)
        x_own[pl.ds(p, n)] = both[:, 0]
        for d in (2, 1, 3):
            x_out[d - 1, pl.ds(p, n)] = both[:, d].astype(BF16)
            sends.append(
                send(
                    x_out.at[d - 1, pl.ds(p, n)], x_in.at[NX - d - 1, pl.ds(p, n)],
                    rx_s.at[g, d - 1], rx_r.at[g, NX - d - 1], device(0, d, 0),
                )
            )
    for p in range(15):
        take(meta.at[p], am_r.at[p])
    for g, (p, n) in enumerate(FAR):
        if g < BACK_DIRECT:
            for dx, dc in plane:
                take(late_in.at[dc, dx, pl.ds(p - BACK_LATE, n)], rl_r.at[g, dc, dx])
        else:
            for d in range(1, NX):
                take(x_in.at[d - 1, pl.ds(p, n)], rx_r.at[g, d - 1])
        for q in range(p, p + n):
            if g < BACK_DIRECT:
                total = stage[pl.ds(q * NX * SUB, SUB), :]
                for dx, dc in plane:
                    total += late_in[dc, dx, q - BACK_LATE].astype(F32)
            else:
                total = x_own[q]
                for d in range(1, NX):
                    total += x_in[d - 1, q].astype(F32)
            factor = jnp.sum(jnp.where(lane == z, meta[q], 0.0), axis=1, keepdims=True)
            total *= factor
            if q == 15:
                x_own[q] = total
            else:
                k = K_OF[q]
                there = P_OF[NZ - k]
                z_out[q] = total.astype(BF16)
                sends.append(send(z_out.at[q], z_in.at[there], rz_s.at[q], rz_r.at[there], device(k, 0, 0)))
    for copy in sends[:-15]:
        copy.wait_send()
    total = x_own[15]
    for p in range(15):
        take(z_in.at[p], rz_r.at[p])
        total += z_in[p].astype(F32)
    out_ref[...] = total.astype(BF16)
    for copy in sends[-15:]:
        copy.wait_send()


def shards(tokens, expert_ids, gates, gate_weight, up_weight, down_weight):
    hidden_dev, width = gate_weight.shape[1:]
    sems = pltpu.SemaphoreType.DMA
    vmem = pl.BlockSpec(memory_space=pltpu.VMEM)
    hbm = pl.BlockSpec(memory_space=pl.ANY)
    result = pl.pallas_call(
        kernel,
        name="routed_experts",
        out_shape=pltpu.VMEM((SUB, LANE), BF16),
        in_specs=[hbm] * 6,
        out_specs=vmem,
        scratch_shapes=[
            pltpu.VMEM((1, width), BF16),
            pltpu.VMEM(expert_ids.shape, jnp.int32),
            pltpu.VMEM(gates.shape, F32),
            pltpu.VMEM((hidden_dev, width), BF16),
            pltpu.VMEM((hidden_dev, width), BF16),
            pltpu.VMEM((hidden_dev, width), BF16),
            pltpu.VMEM((SUB, LANE), BF16),
            pltpu.VMEM((NC, NZ, NX, SUB, LANE), BF16),
            pltpu.VMEM((NZ, 1, LANE), F32),
            pltpu.VMEM((129 * SUB, LANE), F32),
            pltpu.VMEM((128, width), BF16),
            pltpu.VMEM((NZ, NX, SUB, LANE), BF16),
            pltpu.VMEM((NZ, NX, SUB, LANE), BF16),
            pltpu.VMEM((NX - 1, NZ, SUB, LANE), BF16),
            pltpu.VMEM((NX - 1, NZ, SUB, LANE), BF16),
            pltpu.VMEM((NC, NX, SLOTS, SUB, LANE), BF16),
            pltpu.VMEM((NC, NX, SLOTS, SUB, LANE), BF16),
            pltpu.VMEM((NZ, SUB, LANE), F32),
            pltpu.VMEM((NZ - 1, SUB, LANE), BF16),
            pltpu.VMEM((NZ - 1, SUB, LANE), BF16),
            sems((6,)),
            sems((15,)), sems((15,)), sems((15,)), sems((15,)),
            sems((9, NC, NX)), sems((9, NC, NX)), sems((9,)), sems((9,)),
            sems((9,)), sems((9,)), sems((9, 3)), sems((9, 3)),
            sems((max(BACK_DIRECT, 1), NC, NX)), sems((max(BACK_DIRECT, 1), NC, NX)),
            sems((15,)), sems((15,)),
        ],
        compiler_params=pltpu.CompilerParams(collective_id=0, has_side_effects=True),
    )(tokens, expert_ids, gates, gate_weight, up_weight, down_weight)
    return result.reshape(1, width)


def solution(mesh):
    return jax.shard_map(
        shards,
        mesh=mesh,
        in_specs=(
            P(("dp", "ep"), None),
            P(("dp", "ep"), None),
            P(("dp", "ep"), None),
            P("ep", None, None),
            P("ep", None, None),
            P("ep", None, None),
        ),
        out_specs=P(("dp", "ep"), None),
        check_vma=False,
    )
```

```python
import functools

import jax
import jax.numpy as jnp
from jax import lax
from jax.experimental import pallas as pl
from jax.experimental.pallas import tpu as pltpu
from jax.sharding import PartitionSpec as P

MESH = pl.DeviceIdType.MESH
F32 = jnp.float32
BF16 = jnp.bfloat16
NZ, NX, NC = 16, 4, 2
SUB, LANE = 32, 128

K_OF = [k for j in range(1, 8) for k in (j, NZ - j)] + [8, 0]
P_OF = {k: p for p, k in enumerate(K_OF)}
NEAR = [(15, 1)] + [(2 * j, 2) for j in range(7)] + [(14, 1)]
FAR = NEAR[::-1]
OUT_DIRECT = 2
BACK_DIRECT = 1
BACK_LATE = ([(14, 0)] + FAR)[BACK_DIRECT][0]
SLOTS = 15 - BACK_LATE
LEG = 3


def kernel(
    tok_hbm, ids_hbm, gate_hbm, wg_hbm, wu_hbm, wd_hbm, out_ref,
    tok_ref, ids_ref, gate_ref, wg, wu, wd, own, got, meta, stage, rows,
    core_out, core_in, x_out, x_in, late_out, late_in, x_own, z_out, z_in,
    w_sem, az_s, az_r, am_s, am_r, ax_s, ax_r, ac_s, ac_r, rc_s, rc_r, rx_s, rx_r, rl_s, rl_r, rz_s, rz_r,
):
    me = lax.axis_index("ep")
    core = lax.rem(me, NC)
    x = lax.rem(me // NC, NX)
    z = me // (NC * NX)

    def device(dz, dx, dc):
        pz = lax.rem(z + dz, NZ)
        px = lax.rem(x + dx, NX)
        pc = lax.rem(core + dc, NC)
        return {"ep": (pz * NX + px) * NC + pc}

    def send(src, dst, s_sem, r_sem, to):
        copy = pltpu.make_async_remote_copy(
            src_ref=src, dst_ref=dst, send_sem=s_sem, recv_sem=r_sem, device_id=to, device_id_type=MESH
        )
        copy.start()
        return copy

    plane = [(dx, dc) for dc in range(NC) for dx in range(NX)][1:]
    late_order = [(2, 1), (2, 0), (1, 1), (3, 1), (1, 0), (3, 0), (0, 1)]
    peers = [device(s * d % NZ, 0, 0) for d in range(1, LEG + 1) for s in (1, -1)] + [device(0, dx, dc) for dx, dc in plane]
    barrier = pltpu.get_barrier_semaphore()
    for peer in peers:
        pl.semaphore_signal(barrier, inc=1, device_id=peer, device_id_type=MESH)

    loads = []
    for n, (src, dst) in enumerate(
        (
            (tok_hbm, tok_ref), (ids_hbm, ids_ref), (gate_hbm, gate_ref),
            (wg_hbm.at[0], wg), (wu_hbm.at[0], wu), (wd_hbm.at[0], wd),
        )
    ):
        copy = pltpu.make_async_copy(src, dst, w_sem.at[n])
        copy.start()
        loads.append(copy)
    for copy in loads[:3]:
        copy.wait()

    lane = lax.broadcasted_iota(jnp.int32, (1, LANE), 1)
    row = tok_ref[...].astype(F32)
    for j in range(SUB):
        stage[j : j + 1, :] = row[:, j * LANE : (j + 1) * LANE]
    own_row = stage[0:SUB, :].astype(BF16)
    own[...] = own_row
    got[0, 15, 0] = own_row
    weight = jnp.zeros((1, LANE), F32)
    for k in range(ids_ref.shape[1]):
        weight += jnp.where(lane == ids_ref[:, k : k + 1], gate_ref[:, k : k + 1], 0.0)
    meta[15] = weight

    pl.semaphore_wait(barrier, len(peers))

    sends = []
    for d in range(LEG, 0, -1):
        for step in (d, NZ - d):
            p = P_OF[NZ - step]
            sends.append(send(own, got.at[0, p, 0], az_s.at[p], az_r.at[p], device(step, 0, 0)))

    def gates_along_z():
        for d in range(1, NZ):
            p = P_OF[NZ - d]
            sends.append(send(meta.at[15], meta.at[p], am_s.at[p], am_r.at[p], device(d, 0, 0)))

    def take(dst, r_sem):
        pltpu.make_async_copy(dst, dst, r_sem).wait()

    def rows_along_x(g):
        p, n = NEAR[g]
        if g not in (0, LEG):
            for q in range(p, p + n):
                take(got.at[0, q, 0], az_r.at[q])
        for dx, dc in late_order if g > 8 - OUT_DIRECT else ((2, 0), (1, 0), (3, 0)):
            px = (NX - dx) % NX
            sends.append(
                send(
                    got.at[0, pl.ds(p, n), 0], got.at[dc, pl.ds(p, n), px],
                    ax_s.at[g, dc, dx], ax_r.at[g, dc, px], device(0, dx, dc),
                )
            )

    def hand_on():
        below, above = P_OF[NZ - LEG], P_OF[LEG]
        take(got.at[0, below, 0], az_r.at[below])
        take(got.at[0, above, 0], az_r.at[above])
        for m in range(NZ // 2 - LEG, 0, -1):
            hops = [(below, m)] if LEG + m == NZ // 2 else [(below, m), (above, NZ - m)]
            for held, step in hops:
                p = P_OF[(K_OF[held] - step) % NZ]
                sends.append(send(got.at[0, held, 0], got.at[0, p, 0], az_s.at[p], az_r.at[p], device(step, 0, 0)))

    def rows_to_partner(g):
        p, n = NEAR[g]
        for d in range(1, NX):
            take(got.at[0, pl.ds(p, n), d], ax_r.at[g, 0, d])
        sends.append(send(got.at[0, pl.ds(p, n)], got.at[1, pl.ds(p, n)], ac_s.at[g], ac_r.at[g], device(0, 0, 1)))

    def unpack(side, unit):
        base = side * 64 + unit * 16
        stage[pl.ds(base * SUB, 16 * SUB), :] = (
            got[side, 4 * unit : 4 * unit + 4].astype(F32).reshape(16 * SUB, LANE)
        )
        for j in range(SUB):
            rows[pl.ds(base, 16), j * LANE : (j + 1) * LANE] = stage[
                pl.ds(base * SUB + j, 16, stride=SUB), :
            ].astype(BF16)

    def rows_from_partner(g):
        p, n = NEAR[g]
        take(got.at[1, pl.ds(p, n)], ac_r.at[g])

    def late_rows(g):
        p, n = NEAR[g]
        for dx, dc in plane:
            take(got.at[dc, pl.ds(p, n), dx], ax_r.at[g, dc, dx])

    for g in range(LEG):
        rows_along_x(g)
    hand_on()
    for g in range(LEG, 9):
        rows_along_x(g)
    gates_along_z()
    for g in range(5):
        rows_to_partner(g)
    unpack(0, 0)
    rows_to_partner(5)
    unpack(0, 1)
    rows_to_partner(6)
    unpack(0, 2)
    rows_from_partner(1)
    rows_from_partner(2)
    unpack(1, 0)
    rows_from_partner(3)
    rows_from_partner(4)
    unpack(1, 1)
    if OUT_DIRECT < 2:
        rows_to_partner(7)
    rows_from_partner(5)
    rows_from_partner(6)
    unpack(1, 2)
    rows_from_partner(0)
    for g in range(9 - OUT_DIRECT, 9):
        late_rows(g)
    unpack(0, 3)
    if OUT_DIRECT < 2:
        rows_from_partner(7)
    if OUT_DIRECT < 1:
        rows_to_partner(8)
        rows_from_partner(8)
    unpack(1, 3)

    for copy in loads[3:]:
        copy.wait()
    contract = (((1,), (1,)), ((), ()))
    gate_act = lax.dot_general(rows[...], wg[...], contract, preferred_element_type=F32)
    up_act = lax.dot_general(rows[...], wu[...], contract, preferred_element_type=F32)
    hidden = (jax.nn.silu(gate_act) * up_act).astype(BF16)

    def down(blocks):
        size = blocks[0][1] - blocks[0][0]
        some = jnp.concatenate([hidden[first:last] for first, last in blocks], axis=0)
        for n in range(16):
            value = jnp.dot(some, wd[:, n * 256 : (n + 1) * 256], preferred_element_type=F32)
            for b, (first, _) in enumerate(blocks):
                part = value[b * size : (b + 1) * size]
                stage[pl.ds(first * SUB + 2 * n, size, stride=SUB), :] = part[:, :LANE]
                stage[pl.ds(first * SUB + 2 * n + 1, size, stride=SUB), :] = part[:, LANE:]

    down([(48, 64), (112, 128)])
    for g, (p, n) in enumerate(FAR[:BACK_DIRECT]):
        for dx, dc in late_order:
            px = (NX - dx) % NX
            for q in range(n):
                row = ((dc * NZ + p + q) * NX + dx) * SUB
                late_out[dc, dx, p - BACK_LATE + q] = stage[pl.ds(row, SUB), :].astype(BF16)
            sends.append(
                send(
                    late_out.at[dc, dx, pl.ds(p - BACK_LATE, n)], late_in.at[dc, px, pl.ds(p - BACK_LATE, n)],
                    rl_s.at[g, dc, dx], rl_r.at[g, dc, px], device(0, dx, dc),
                )
            )
    for g, (p, n) in enumerate(FAR):
        if g == 2:
            down([(0, 48), (64, 112)])
        if g < BACK_DIRECT:
            continue
        core_out[pl.ds(p, n)] = (
            stage[pl.ds((64 + p * 4) * SUB, n * 4 * SUB), :].astype(BF16).reshape(n, NX, SUB, LANE)
        )
        sends.append(send(core_out.at[pl.ds(p, n)], core_in.at[pl.ds(p, n)], rc_s.at[g], rc_r.at[g], device(0, 0, 1)))
    for g, (p, n) in enumerate(FAR):
        if g < BACK_DIRECT:
            continue
        take(core_in.at[pl.ds(p, n)], rc_r.at[g])
        mine = stage[pl.ds(p * 4 * SUB, n * 4 * SUB), :].reshape(n, NX, SUB, LANE)
        both = mine + core_in[pl.ds(p, n)].astype(F32)
        x_own[pl.ds(p, n)] = both[:, 0]
        for d in (2, 1, 3):
            x_out[d - 1, pl.ds(p, n)] = both[:, d].astype(BF16)
            sends.append(
                send(
                    x_out.at[d - 1, pl.ds(p, n)], x_in.at[NX - d - 1, pl.ds(p, n)],
                    rx_s.at[g, d - 1], rx_r.at[g, NX - d - 1], device(0, d, 0),
                )
            )
    for p in range(15):
        take(meta.at[p], am_r.at[p])
    factors = [jnp.sum(jnp.where(lane == z, meta[p], 0.0), axis=1, keepdims=True) for p in range(NZ)]
    for g, (p, n) in enumerate(FAR):
        if g < BACK_DIRECT:
            for dx, dc in plane:
                take(late_in.at[dc, dx, pl.ds(p - BACK_LATE, n)], rl_r.at[g, dc, dx])
        else:
            for d in range(1, NX):
                take(x_in.at[d - 1, pl.ds(p, n)], rx_r.at[g, d - 1])
        for q in range(p, p + n):
            if g < BACK_DIRECT:
                total = stage[pl.ds(q * NX * SUB, SUB), :]
                for dx, dc in plane:
                    total += late_in[dc, dx, q - BACK_LATE].astype(F32)
            else:
                total = x_own[q]
                for d in range(1, NX):
                    total += x_in[d - 1, q].astype(F32)
            total *= factors[q]
            if q == 15:
                x_own[q] = total
            else:
                k = K_OF[q]
                there = P_OF[NZ - k]
                z_out[q] = total.astype(BF16)
                sends.append(send(z_out.at[q], z_in.at[there], rz_s.at[q], rz_r.at[there], device(k, 0, 0)))
    for copy in sends[:-15]:
        copy.wait_send()
    total = x_own[15]
    for p in range(15):
        take(z_in.at[p], rz_r.at[p])
        total += z_in[p].astype(F32)
    out_ref[...] = total.astype(BF16)
    for copy in sends[-15:]:
        copy.wait_send()


def shards(tokens, expert_ids, gates, gate_weight, up_weight, down_weight):
    hidden_dev, width = gate_weight.shape[1:]
    sems = pltpu.SemaphoreType.DMA
    vmem = pl.BlockSpec(memory_space=pltpu.VMEM)
    hbm = pl.BlockSpec(memory_space=pl.ANY)
    result = pl.pallas_call(
        kernel,
        name="routed_experts",
        out_shape=pltpu.VMEM((SUB, LANE), BF16),
        in_specs=[hbm] * 6,
        out_specs=vmem,
        scratch_shapes=[
            pltpu.VMEM((1, width), BF16),
            pltpu.VMEM(expert_ids.shape, jnp.int32),
            pltpu.VMEM(gates.shape, F32),
            pltpu.VMEM((hidden_dev, width), BF16),
            pltpu.VMEM((hidden_dev, width), BF16),
            pltpu.VMEM((hidden_dev, width), BF16),
            pltpu.VMEM((SUB, LANE), BF16),
            pltpu.VMEM((NC, NZ, NX, SUB, LANE), BF16),
            pltpu.VMEM((NZ, 1, LANE), F32),
            pltpu.VMEM((128 * SUB, LANE), F32),
            pltpu.VMEM((128, width), BF16),
            pltpu.VMEM((NZ, NX, SUB, LANE), BF16),
            pltpu.VMEM((NZ, NX, SUB, LANE), BF16),
            pltpu.VMEM((NX - 1, NZ, SUB, LANE), BF16),
            pltpu.VMEM((NX - 1, NZ, SUB, LANE), BF16),
            pltpu.VMEM((NC, NX, SLOTS, SUB, LANE), BF16),
            pltpu.VMEM((NC, NX, SLOTS, SUB, LANE), BF16),
            pltpu.VMEM((NZ, SUB, LANE), F32),
            pltpu.VMEM((NZ - 1, SUB, LANE), BF16),
            pltpu.VMEM((NZ - 1, SUB, LANE), BF16),
            sems((6,)),
            sems((15,)), sems((15,)), sems((15,)), sems((15,)),
            sems((9, NC, NX)), sems((9, NC, NX)), sems((9,)), sems((9,)),
            sems((9,)), sems((9,)), sems((9, 3)), sems((9, 3)),
            sems((max(BACK_DIRECT, 1), NC, NX)), sems((max(BACK_DIRECT, 1), NC, NX)),
            sems((15,)), sems((15,)),
        ],
        compiler_params=pltpu.CompilerParams(collective_id=0, has_side_effects=True),
    )(tokens, expert_ids, gates, gate_weight, up_weight, down_weight)
    return result.reshape(1, width)


def solution(mesh):
    return jax.shard_map(
        shards,
        mesh=mesh,
        in_specs=(
            P(("dp", "ep"), None),
            P(("dp", "ep"), None),
            P(("dp", "ep"), None),
            P("ep", None, None),
            P("ep", None, None),
            P("ep", None, None),
        ),
        out_specs=P(("dp", "ep"), None),
        check_vma=False,
    )
```
